256 devices in a mesh: label: 8 (over z_hi, core), seq: 32 (over y, x, z_lo).
Axes of the slice: x: 4, y: 4, z: 8 (z_hi: 4, z_lo: 2; z = z_hi * 2 + z_lo), core: 2. Of those that a mesh axis runs over, the one named last changes fastest.
Arguments:
- hidden: bfloat16 [32768, 1024], P('seq'), may hold values from -8 to 8
- slot_note: int32 [32768], P('seq'), may hold values from 0 to 8, as said below
- queries: bfloat16 [4096, 1024], P('label'), may hold values from -64 to 64
- out_vectors: bfloat16 [4096, 1024], P('label'), may hold values from -0.1875 to 0.1875
- label_bias: float32 [4096], P('label'), may hold values from -3 to 1
- targets: int32 [8, 4096], P(None, 'label'), may hold values 0 or 1
Outputs:
- token_grad: bfloat16 [32768, 1024], P('seq', 'label')
- query_grad: float32 [4096, 1024], P(('label', 'seq'))
- out_grad: float32 [4096, 1024], P(('label', 'seq'))
The draws below stay inside these ranges and needn't reach their ends.
Inputs may be any that keep to these rules, and one draw needn't show every extreme that they name: `slot_note`: on each index of seq the filled slots come first. Over filled slots, in the order of seq indices and then slots, note numbers never fall, and every note has at least one filled slot. The seq indices i and i + 32 / 2 together hold at most 1024 filled slots, and some such pair holds exactly 1024.
All inputs are finite; a program needn't handle non-finite values. No bound on the sum of `targets` on one device may be relied on, other than what follows from the above.
Results may differ from the reference program's by a relative error of at most 0.0049.
Values may be sent and summed in bfloat16 or wider, within the bound.
No kernel may reach another device: no remote copies, remote signals or barrier semaphores. Data moves between devices by JAX's collectives and lax.ppermute only.
A program may use at most 64 MiB of HBM per device.

```python
import math
import jax
import jax.numpy as jnp
from jax import lax

D = 1024
LAB_DEV = 512
TOK_DEV = 1024
NOTES = 8
LABELS = 4096
TOKENS = 32768
N_LABEL = 8
N_SEQ = 32


def layout_draw(key):
    stream = jax.random.fold_in(key, 11)
    keys = jax.random.split(stream, 4)
    pairs = N_SEQ // 2
    pair_total = jax.random.randint(keys[0], (pairs,), TOK_DEV // 4, 3 * TOK_DEV // 4 + 1)
    forced = jax.random.randint(keys[1], (), 0, pairs)
    is_forced = jnp.arange(pairs) == forced
    pair_total = jnp.where(is_forced, TOK_DEV, pair_total)
    lower_count = jax.random.randint(keys[2], (pairs,), 0, pair_total + 1)
    lower_count = jnp.where(is_forced, TOK_DEV, lower_count)
    counts = jnp.concatenate([lower_count, pair_total - lower_count])
    offsets = jnp.cumsum(counts) - counts
    slot_index = jnp.arange(TOK_DEV)
    filled = slot_index[None, :] < counts[:, None]
    ranks = offsets[:, None] + slot_index[None, :]
    total = jnp.sum(counts)
    widths = jax.random.randint(keys[3], (NOTES,), 1, 5)
    bounds = jnp.cumsum(widths)
    cuts = bounds[:-1] * total // bounds[-1]
    note_ids = jnp.sum(ranks[:, :, None] >= cuts[None, None, :], axis=-1)
    slots = jnp.where(filled, note_ids, NOTES).reshape(-1).astype(jnp.int32)
    return slots


def token_rows(key):
    stream = jax.random.fold_in(key, 23)
    second_key = jax.random.fold_in(stream, 1)
    return jnp.clip(jax.random.normal(second_key, (TOKENS, D)), -4.0, 4.0)


def draw_slot_note(key, part):
    slots = layout_draw(key)
    return slots


def draw_hidden(key, part):
    return token_rows(key).astype(jnp.bfloat16)


def draw_queries(key, part):
    stream = jax.random.fold_in(key, 37)
    return (jnp.clip(jax.random.normal(stream, (LABELS, D)), -4.0, 4.0) / math.sqrt(D)).astype(jnp.bfloat16)


def plant(array, rng, low, high):
    index_at = [jax.random.randint(jax.random.fold_in(rng, axis), (), 0, length) for axis, length in enumerate(array.shape)]
    main_axis = array.shape.index(max(array.shape))
    next_to = index_at[:main_axis] + [(index_at[main_axis] + 1) % array.shape[main_axis]] + index_at[main_axis + 1:]
    return array.at[tuple(index_at)].set(low).at[tuple(next_to)].set(high)


def block_levels(own_key, shape, cuts, least, high):
    def one(axis_at, parts):
        draws = jax.random.uniform(jax.random.fold_in(jax.random.fold_in(own_key, 6), axis_at), (parts,), jnp.float32, least / len(cuts), high / len(cuts))
        return jnp.repeat(jnp.exp(draws), shape[axis_at] // parts).reshape((-1,) + (1,) * (len(shape) - axis_at - 1))

    gain = one(*cuts[0])
    for cut in cuts[1:]:
        gain = gain * one(*cut)
    return gain


def centred(stream_key, shape, spread, most, cuts=(), kind=jnp.bfloat16):
    entries = spread * jax.random.normal(stream_key, shape, jnp.float32)
    if cuts:
        entries = entries * block_levels(stream_key, shape, cuts, -0.22, 0.18)
    return jnp.clip(entries, -most, most).astype(kind)


def setup_inputs(seed: int = 0) -> dict:
    streams_of = jax.random.split(jax.random.key(seed), 7)
    return {
        "hidden": draw_hidden(jax.random.fold_in(streams_of[6], 71), 0),
        "slot_note": draw_slot_note(jax.random.fold_in(streams_of[6], 71), 0),
        "queries": draw_queries(jax.random.fold_in(streams_of[6], 71), 0),
        "out_vectors": centred(streams_of[3], (LABELS, D), D ** -0.5, 0.1875, ((0, 8),)),
        "label_bias": jnp.clip(-3.0 + 4.0 * jax.random.uniform(streams_of[4], (LABELS,), jnp.float32) ** block_levels(streams_of[4], (LABELS,), ((0, 8),), -0.2, 0.2), -3.0, 1.0),
        "targets": plant((jax.random.randint(streams_of[5], (NOTES, LABELS), 0, 8) < 1).astype(jnp.int32), jax.random.fold_in(streams_of[5], 1), 0, 1),
    }


MASKED_SCORE = -1.0e30
LOSS_SCALE = 256.0


def reference(hidden, slot_note, queries, out_vectors, label_bias, targets):
    note_ids = jnp.arange(NOTES, dtype=jnp.int32)
    onehot = (slot_note[:, None] == note_ids[None, :]).astype(jnp.float32)
    filled = slot_note < NOTES
    hidden_t = hidden.T
    query_blocks = queries.reshape(N_LABEL, LAB_DEV, D)
    vector_blocks = out_vectors.reshape(N_LABEL, LAB_DEV, D)
    bias_blocks = label_bias.reshape(N_LABEL, LAB_DEV)
    target_blocks = targets.T.astype(jnp.float32).reshape(N_LABEL, LAB_DEV, NOTES)

    def label_block(running, blocks):
        query_block, vector_block, bias_block, target_block = blocks
        stacked = jnp.concatenate([query_block, vector_block], axis=0)
        products = jnp.dot(stacked, hidden_t, preferred_element_type=jnp.float32)
        scores = products[:LAB_DEV]
        gain_rows = products[LAB_DEV:]
        note_top = jnp.stack([jnp.max(jnp.where(slot_note[None, :] == note_id, scores, MASKED_SCORE), axis=1) for note_id in range(NOTES)], axis=1)
        top_rows = jnp.dot(note_top, onehot.T, precision=lax.Precision.HIGHEST)
        expo_rows = jnp.exp(jnp.where(filled[None, :], scores - top_rows, -jnp.inf))
        weight_sum = jnp.dot(expo_rows, onehot, precision=lax.Precision.HIGHEST)
        gain_sum = jnp.dot(expo_rows * gain_rows, onehot, precision=lax.Precision.HIGHEST)
        context = gain_sum / weight_sum
        dlogit = LOSS_SCALE * (jax.nn.sigmoid(context + bias_block[:, None]) - target_block)
        tables = jnp.dot(jnp.concatenate([dlogit / weight_sum, context], axis=0), onehot.T, precision=lax.Precision.HIGHEST)
        out_coef = expo_rows * tables[:LAB_DEV]
        query_coef = out_coef * (gain_rows - tables[LAB_DEV:])
        coefficients = jnp.concatenate([query_coef, out_coef], axis=0).astype(jnp.bfloat16)
        token_term = lax.dot_general(coefficients, stacked, (((0,), (0,)), ((), ())), preferred_element_type=jnp.float32)
        gradients = jnp.dot(coefficients, hidden, preferred_element_type=jnp.float32)
        return running + token_term, gradients

    start_total = jnp.zeros((hidden.shape[0], D), jnp.float32)
    token_total, gradients = lax.scan(label_block, start_total, (query_blocks, vector_blocks, bias_blocks, target_blocks))
    query_grad = gradients[:, :LAB_DEV].reshape(N_LABEL * LAB_DEV, D)
    out_grad = gradients[:, LAB_DEV:].reshape(N_LABEL * LAB_DEV, D)
    return token_total.astype(jnp.bfloat16), query_grad, out_grad
```

```python
import jax
import jax.numpy as jnp
from jax import lax
from jax.experimental import pallas as pl
from jax.experimental.pallas import tpu as pltpu
from jax.sharding import Mesh
from jax.sharding import PartitionSpec as P

MASKED_SCORE = -1e30
LOSS_SCALE = 256.0
ROWS = 64
MIB = 1 << 20


VMEM = pl.BlockSpec(memory_space=pltpu.VMEM)
SMEM = pl.BlockSpec(memory_space=pltpu.SMEM)


def note_starts(notes_ref, slots, note_count):
    starts = [jnp.int32(0)]
    for note in range(1, note_count + 1):
        at = jnp.int32(0)
        step = slots // 2
        while step:
            at = jnp.where(notes_ref[at + (step - 1)] < note, at + step, at)
            step //= 2
        starts.append(jnp.where(notes_ref[at] < note, at + 1, at))
    return starts


def stats_kernel(notes_ref, h_ref, q_ref, o_ref, expo_ref, gain_ref, table_ref, start_ref, tops, weights, gains):
    slots, labels = expo_ref.shape
    note_count = table_ref.shape[0] // 3
    block = h_ref.shape[0]
    step = pl.program_id(0)
    rows = pl.ds(pl.multiple_of(step * block, block), block)
    contract = (((1,), (1,)), ((), ()))
    expo_ref[rows, :] = lax.dot_general(h_ref[...], q_ref[...], contract, preferred_element_type=jnp.float32)
    gain_ref[rows, :] = lax.dot_general(h_ref[...], o_ref[...], contract, preferred_element_type=jnp.float32)

    @pl.when(step == pl.num_programs(0) - 1)
    def _():
        for note, start in enumerate(note_starts(notes_ref, slots, note_count)):
            start_ref[note] = start
        start_ref[note_count + 1] = jnp.int32(slots)
        tops[...] = jnp.full(tops.shape, MASKED_SCORE, jnp.float32)
        weights[...] = jnp.zeros(weights.shape, jnp.float32)
        gains[...] = jnp.zeros(gains.shape, jnp.float32)
        row = lax.broadcasted_iota(jnp.int32, (ROWS, labels), 0)

        def fold(values, how):
            return how(values.reshape(ROWS // 8, 8, labels), axis=0)

        def top_block(index, carry):
            first = index * ROWS
            at = pl.ds(pl.multiple_of(first, ROWS), ROWS)
            scores = expo_ref[at, :]

            def one(note, carry):
                inside = (row >= start_ref[note] - first) & (row < start_ref[note + 1] - first)
                tops[note] = jnp.maximum(tops[note], fold(jnp.where(inside, scores, MASKED_SCORE), jnp.max))
                return carry

            return lax.fori_loop(notes_ref[first], notes_ref[first + ROWS - 1] + 1, one, carry)

        lax.fori_loop(0, slots // ROWS, top_block, 0)
        for note in range(note_count):
            top = jnp.max(tops[note], axis=0, keepdims=True)
            table_ref[note : note + 1, :] = top
            tops[note] = jnp.broadcast_to(top, (8, labels))
        tops[note_count] = jnp.full((8, labels), -MASKED_SCORE, jnp.float32)

        def expo_block(index, carry):
            first = index * ROWS
            at = pl.ds(pl.multiple_of(first, ROWS), ROWS)

            def one(note, carry):
                inside = (row >= start_ref[note] - first) & (row < start_ref[note + 1] - first)
                scores = expo_ref[at, :]
                shift = scores.reshape(ROWS // 8, 8, labels) - tops[note][None]
                expo = jnp.exp(shift).reshape(ROWS, labels)
                expo_ref[at, :] = jnp.where(inside, expo, scores)
                expo = jnp.where(inside, expo, 0.0)
                weights[note] += fold(expo, jnp.sum)
                gains[note] += fold(expo * gain_ref[at, :], jnp.sum)
                return carry

            return lax.fori_loop(notes_ref[first], notes_ref[first + ROWS - 1] + 1, one, carry)

        lax.fori_loop(0, slots // ROWS, expo_block, 0)
        for note in range(note_count):
            table_ref[note_count + note : note_count + note + 1, :] = jnp.sum(weights[note], axis=0, keepdims=True)
            table_ref[2 * note_count + note : 2 * note_count + note + 1, :] = jnp.sum(gains[note], axis=0, keepdims=True)


def local_stats(notes, hidden, queries, out_vectors, note_count):
    slots, width = hidden.shape
    labels = queries.shape[0]
    block = 256
    wide = jax.ShapeDtypeStruct((slots, labels), jnp.float32)
    whole = pl.BlockSpec((labels, width), lambda i: (0, 0))
    return pl.pallas_call(
        stats_kernel,
        out_shape=(
            wide,
            wide,
            jax.ShapeDtypeStruct((3 * note_count, labels), jnp.float32),
            jax.ShapeDtypeStruct((2 * note_count,), jnp.int32),
        ),
        grid=(slots // block,),
        in_specs=[SMEM, pl.BlockSpec((block, width), lambda i: (i, 0)), whole, whole],
        out_specs=(VMEM, VMEM, VMEM, SMEM),
        scratch_shapes=[pltpu.VMEM((note_count + 1, 8, labels), jnp.float32)] * 3,
        compiler_params=pltpu.CompilerParams(vmem_limit_bytes=24 * MIB),
        name="local_stats",
    )(notes, hidden, queries, out_vectors)


def merged(tables):
    n = tables[0].shape[0] // 3
    top = tables[0][:n]
    for table in tables[1:]:
        top = jnp.maximum(top, table[:n])
    weight = gain = 0.0
    for table in tables:
        scale = jnp.exp(table[:n] - top)
        weight = weight + scale * table[n : 2 * n]
        gain = gain + scale * table[2 * n :]
    return top, weight, gain


def merge_kernel(*refs):
    n = refs[0].shape[0] // 3
    out = refs[-1]
    out[:n], out[n : 2 * n], out[2 * n :] = merged([ref[...] for ref in refs[:-1]])


def merge(tables):
    return pl.pallas_call(
        merge_kernel,
        out_shape=jax.ShapeDtypeStruct(tables[0].shape, jnp.float32),
        in_specs=[VMEM] * len(tables),
        out_specs=VMEM,
        compiler_params=pltpu.CompilerParams(vmem_limit_bytes=2 * MIB),
        name="merge",
    )(*tables)


def coef_kernel(notes_ref, start_ref, expo_ref, gain_ref, local_ref, a_ref, b_ref, bias_ref, target_ref, h_ref,
                query_ref, out_ref, label_ref, scale_rows, context_rows):
    slots, labels = expo_ref.shape
    note_count = target_ref.shape[0]
    top, weight, gain = merged([a_ref[...], b_ref[...]])
    context = gain / weight
    chance = 1.0 / (1.0 + jnp.exp(-(context + bias_ref[...])))
    dlogit = LOSS_SCALE * (chance - target_ref[...].astype(jnp.float32))
    scale = jnp.exp(local_ref[:note_count] - top) * (dlogit / weight)
    for note in range(note_count):
        scale_rows[note] = jnp.broadcast_to(scale[note : note + 1], (8, labels))
        context_rows[note] = jnp.broadcast_to(context[note : note + 1], (8, labels))
    scale_rows[note_count] = jnp.zeros((8, labels), jnp.float32)
    context_rows[note_count] = jnp.zeros((8, labels), jnp.float32)
    row = lax.broadcasted_iota(jnp.int32, (ROWS, labels), 0)

    def block(index, carry):
        first = index * ROWS
        at = pl.ds(pl.multiple_of(first, ROWS), ROWS)

        def one(note, carry):
            since = row >= start_ref[note] - first
            shape = (ROWS // 8, 8, labels)
            out = expo_ref[at, :].reshape(shape) * scale_rows[note][None]
            query = out * (gain_ref[at, :].reshape(shape) - context_rows[note][None])
            for ref, new in ((query_ref, query), (out_ref, out)):
                old = ref[at, :].astype(jnp.float32)
                ref[at, :] = jnp.where(since, new.reshape(ROWS, labels), old).astype(jnp.bfloat16)
            return carry

        return lax.fori_loop(notes_ref[first], notes_ref[first + ROWS - 1] + 1, one, carry)

    lax.fori_loop(0, slots // ROWS, block, 0)
    width = h_ref.shape[1]
    part = 128
    for side, ref in enumerate((query_ref, out_ref)):
        for k in range(labels // part):
            some = ref[:, k * part : (k + 1) * part]
            total = lax.dot_general(some, h_ref[...], (((0,), (0,)), ((), ())), preferred_element_type=jnp.float32)
            label_ref[k * part : (k + 1) * part, side * width : (side + 1) * width] = total.astype(jnp.bfloat16)


def coefficients(notes, starts, expo, gain, local, a, b, bias, targets, hidden):
    slots, labels = expo.shape
    width = hidden.shape[1]
    note_count = targets.shape[0]
    narrow = jax.ShapeDtypeStruct((slots, labels), jnp.bfloat16)
    return pl.pallas_call(
        coef_kernel,
        out_shape=(narrow, narrow, jax.ShapeDtypeStruct((labels, 2 * width), jnp.bfloat16)),
        in_specs=[SMEM, SMEM] + [VMEM] * 8,
        out_specs=(VMEM, VMEM, VMEM),
        scratch_shapes=[pltpu.VMEM((note_count + 1, 8, labels), jnp.float32)] * 2,
        compiler_params=pltpu.CompilerParams(vmem_limit_bytes=24 * MIB),
        name="coefficients",
    )(notes, starts, expo, gain, local, a, b, bias, targets, hidden)


def token_kernel(place_ref, cq_ref, co_ref, q_ref, o_ref, mine_ref, theirs_ref):
    total = jnp.dot(cq_ref[...], q_ref[...], preferred_element_type=jnp.float32)
    total += jnp.dot(co_ref[...], o_ref[...], preferred_element_type=jnp.float32)
    half = total.shape[1] // 2
    low = total[:, :half].astype(jnp.bfloat16)
    high = total[:, half:].astype(jnp.bfloat16)

    @pl.when(place_ref[1] == 0)
    def _():
        mine_ref[...] = low
        theirs_ref[...] = high

    @pl.when(place_ref[1] != 0)
    def _():
        mine_ref[...] = high
        theirs_ref[...] = low


def token_terms(place, query_coef, out_coef, queries, out_vectors, groups):
    slots, labels = query_coef.shape
    width = queries.shape[1]
    pair = width // groups
    half = pair // 2
    coef = pl.BlockSpec((slots, labels), lambda d, place: (0, 0))
    weight = pl.BlockSpec((labels, pair), lambda d, place: (0, lax.rem(place[0] + d, groups)))
    out = pl.BlockSpec((None, slots, half), lambda d, place: (d, 0, 0))
    shape = jax.ShapeDtypeStruct((groups, slots, half), jnp.bfloat16)
    return pl.pallas_call(
        token_kernel,
        out_shape=(shape, shape),
        grid_spec=pltpu.PrefetchScalarGridSpec(
            num_scalar_prefetch=1, grid=(groups,), in_specs=[coef, coef, weight, weight], out_specs=(out, out)
        ),
        compiler_params=pltpu.CompilerParams(vmem_limit_bytes=24 * MIB),
        name="token_terms",
    )(place, query_coef, out_coef, queries, out_vectors)


def shift(value, axis, by):
    size = lax.axis_size(axis)
    return lax.ppermute(value, axis, [(i, (i + by) % size) for i in range(size)])


def shards(hidden, slot_note, queries, out_vectors, label_bias, targets):
    note_count, labels = targets.shape
    width = queries.shape[1]
    f32, bf16 = jnp.float32, jnp.bfloat16
    expo, gain, local, starts = local_stats(slot_note, hidden, queries, out_vectors, note_count)
    table = local
    for axis in ("x", "y"):
        table = merge([table] + [shift(table, axis, by) for by in range(1, lax.axis_size(axis))])
    other = shift(table, "zlo", 1)
    query_coef, out_coef, label_term = coefficients(
        slot_note, starts, expo, gain, local, table, other, label_bias[None, :], targets, hidden
    )
    groups = lax.axis_size("zhi")
    planes = lax.axis_size("y") * lax.axis_size("x")
    pieces = lax.all_to_all(label_term.reshape(planes, labels // planes, 2 * width), ("y", "x"), 0, 0)

    place = jnp.stack([lax.axis_index("zhi"), lax.axis_index("core")]).astype(jnp.int32)
    mine, theirs = token_terms(place, query_coef, out_coef, queries, out_vectors, groups)
    given = shift(theirs, "core", 1)
    paired = [(mine[d].astype(f32) + given[d].astype(f32)).astype(bf16) for d in range(1, groups)]
    token = mine[0].astype(f32) + given[0].astype(f32)
    for d in range(1, groups):
        token = token + shift(paired[d - 1], "zhi", d).astype(f32)

    rows = labels // planes // 2
    low = lax.axis_index("zlo")

    def total(which):
        return jnp.sum(lax.dynamic_slice_in_dim(pieces, which * rows, rows, 1).astype(f32), axis=0)

    sent = shift(total(1 - low).astype(bf16), "zlo", 1)
    label = total(low) + sent.astype(f32)
    return token.astype(bf16), label[:, :width], label[:, width:]


def solution(mesh):
    split = Mesh(mesh.devices.reshape(4, 2, 4, 4, 2), ("zhi", "core", "y", "x", "zlo"))
    label, seq = ("zhi", "core"), ("y", "x", "zlo")
    in_specs = (P(seq, None), P(seq), P(label, None), P(label, None), P(label), P(None, label))
    out_specs = (P(seq, label), P(label + seq, None), P(label + seq, None))
    return jax.shard_map(shards, mesh=split, in_specs=in_specs, out_specs=out_specs, check_vma=False)
```

```python
import jax
import jax.numpy as jnp
from jax import lax
from jax.experimental import pallas as pl
from jax.experimental.pallas import tpu as pltpu
from jax.sharding import Mesh
from jax.sharding import PartitionSpec as P

MASKED_SCORE = -1e30
LOSS_SCALE = 256.0
ROWS = 64
MIB = 1 << 20


VMEM = pl.BlockSpec(memory_space=pltpu.VMEM)
SMEM = pl.BlockSpec(memory_space=pltpu.SMEM)
HBM = pl.BlockSpec(memory_space=pltpu.HBM)


def in_hbm(value):
    return pltpu.with_memory_space_constraint(value, pltpu.HBM)


RANGES = 16


def note_starts(notes_ref, slots, note_count):
    starts = [jnp.int32(0)]
    for note in range(1, note_count + 1):
        at = jnp.int32(0)
        step = slots // 2
        while step:
            at = jnp.where(notes_ref[at + (step - 1)] < note, at + step, at)
            step //= 2
        starts.append(jnp.where(notes_ref[at] < note, at + 1, at))
    return starts


def fold(values, how):
    rows, labels = values.shape
    return how(values.reshape(rows // 8, 8, labels), axis=0)


def spread(values, rows):
    return jnp.broadcast_to(values[None], (rows // 8,) + values.shape).reshape(rows, values.shape[1])


def by_note(info_ref, slots, one):
    def block(index, carry):
        first = index * ROWS
        at = pl.ds(pl.multiple_of(first, ROWS), ROWS)
        low = info_ref[RANGES + 2 * index]
        high = info_ref[RANGES + 2 * index + 1]

        @pl.when(low == high)
        def _():
            one(at, low, None)

        @pl.when(low != high)
        def _():
            def each(note, carry):
                def mask(shape):
                    row = lax.broadcasted_iota(jnp.int32, shape, 0)
                    return (row >= info_ref[note] - first) & (row < info_ref[note + 1] - first)

                one(at, note, mask)
                return carry

            lax.fori_loop(low, high + 1, each, 0)

        return carry

    lax.fori_loop(0, slots // ROWS, block, 0)


def stats_kernel(notes_hbm, h_hbm, q_hbm, o_hbm, both_ref, table_ref, info_ref, h_ref, w_ref,
                 notes_ref, tops, weights, gains, sems):
    slots = both_ref.shape[0]
    labels = q_hbm.shape[0]
    note_count = table_ref.shape[0] // 3
    part = slots // 2
    copies = [pltpu.make_async_copy(notes_hbm, notes_ref, sems.at[0]),
              pltpu.make_async_copy(q_hbm, w_ref.at[pl.ds(0, labels), :], sems.at[1]),
              pltpu.make_async_copy(o_hbm, w_ref.at[pl.ds(labels, labels), :], sems.at[2])]
    for k in range(2):
        rows = pl.ds(k * part, part)
        copies.append(pltpu.make_async_copy(h_hbm.at[rows, :], h_ref.at[rows, :], sems.at[3 + k]))
    for k in (0, 3, 1, 2, 4):
        copies[k].start()
    tops[...] = jnp.full(tops.shape, MASKED_SCORE, jnp.float32)
    weights[...] = jnp.zeros(weights.shape, jnp.float32)
    gains[...] = jnp.zeros(gains.shape, jnp.float32)
    copies[0].wait()
    for note, start in enumerate(note_starts(notes_ref, slots, note_count)):
        info_ref[note] = start
    info_ref[note_count + 1] = jnp.int32(slots)
    for k in range(slots // ROWS):
        info_ref[RANGES + 2 * k] = notes_ref[k * ROWS]
        info_ref[RANGES + 2 * k + 1] = notes_ref[k * ROWS + ROWS - 1]
    for k in (3, 1, 2, 4):
        copies[k].wait()

    def product(k, carry):
        rows = pl.ds(pl.multiple_of(k * part, part), part)
        both_ref[rows, :] = lax.dot_general(
            h_ref[rows, :], w_ref[...], (((1,), (1,)), ((), ())), preferred_element_type=jnp.float32
        )
        return carry

    lax.fori_loop(0, 2, product, 0)
    left, right = slice(0, labels), slice(labels, 2 * labels)

    def top(at, note, mask):
        scores = both_ref[at, left]
        if mask is not None:
            scores = jnp.where(mask(scores.shape), scores, MASKED_SCORE)
        tops[note] = jnp.maximum(tops[note], fold(scores, jnp.max))

    by_note(info_ref, slots, top)
    for note in range(note_count):
        most = jnp.max(tops[note], axis=0, keepdims=True)
        table_ref[note : note + 1, :] = most
        tops[note] = jnp.broadcast_to(most, (8, labels))
    tops[note_count] = jnp.full((8, labels), -MASKED_SCORE, jnp.float32)

    def exponent(at, note, mask):
        scores = both_ref[at, left]
        expo = jnp.exp(scores - spread(tops[note], ROWS))
        if mask is None:
            both_ref[at, left] = expo
        else:
            inside = mask(scores.shape)
            both_ref[at, left] = jnp.where(inside, expo, scores)
            expo = jnp.where(inside, expo, 0.0)
        weights[note] += fold(expo, jnp.sum)
        gains[note] += fold(expo * both_ref[at, right], jnp.sum)

    by_note(info_ref, slots, exponent)
    for note in range(note_count):
        table_ref[note_count + note : note_count + note + 1, :] = jnp.sum(weights[note], axis=0, keepdims=True)
        table_ref[2 * note_count + note : 2 * note_count + note + 1, :] = jnp.sum(gains[note], axis=0, keepdims=True)


def local_stats(notes, hidden, queries, out_vectors, note_count):
    slots, width = hidden.shape
    labels = queries.shape[0]
    return pl.pallas_call(
        stats_kernel,
        out_shape=(
            pltpu.VMEM((slots, 2 * labels), jnp.float32),
            jax.ShapeDtypeStruct((3 * note_count, labels), jnp.float32),
            jax.ShapeDtypeStruct((RANGES + 2 * (slots // ROWS),), jnp.int32),
            pltpu.VMEM(hidden.shape, hidden.dtype),
            pltpu.VMEM((2 * labels, width), queries.dtype),
        ),
        in_specs=[HBM] * 4,
        out_specs=(VMEM, VMEM, SMEM, VMEM, VMEM),
        scratch_shapes=[pltpu.SMEM((slots,), jnp.int32)]
        + [pltpu.VMEM((note_count + 1, 8, labels), jnp.float32)] * 3
        + [pltpu.SemaphoreType.DMA((5,))],
        compiler_params=pltpu.CompilerParams(vmem_limit_bytes=24 * MIB),
        name="local_stats",
    )(*map(in_hbm, (notes, hidden, queries, out_vectors)))


def merged(tables):
    n = tables[0].shape[0] // 3
    top = tables[0][:n]
    for table in tables[1:]:
        top = jnp.maximum(top, table[:n])
    weight = gain = 0.0
    for table in tables:
        scale = jnp.exp(table[:n] - top)
        weight = weight + scale * table[n : 2 * n]
        gain = gain + scale * table[2 * n :]
    return top, weight, gain


def merge_kernel(*refs):
    n = refs[0].shape[0] // 3
    out = refs[-1]
    out[:n], out[n : 2 * n], out[2 * n :] = merged([ref[...] for ref in refs[:-1]])


def merge(tables):
    return pl.pallas_call(
        merge_kernel,
        out_shape=jax.ShapeDtypeStruct(tables[0].shape, jnp.float32),
        in_specs=[VMEM] * len(tables),
        out_specs=VMEM,
        compiler_params=pltpu.CompilerParams(vmem_limit_bytes=2 * MIB),
        name="merge",
    )(*tables)


def terms_kernel(info_ref, both_ref, local_ref, a_ref, b_ref, bias_ref, target_ref, h_ref, w_ref,
                 label_hbm, mine_hbm, theirs_hbm, coef_ref, label_ref, token_ref, scale_rows, context_rows, sems):
    slots, labels = both_ref.shape[0], bias_ref.shape[1]
    width = h_ref.shape[1]
    note_count = target_ref.shape[0]
    groups = mine_hbm.shape[0]
    left, right = slice(0, labels), slice(labels, 2 * labels)
    top, weight, gain = merged([a_ref[...], b_ref[...]])
    context = gain / weight
    chance = 1.0 / (1.0 + jnp.exp(-(context + bias_ref[...])))
    dlogit = LOSS_SCALE * (chance - target_ref[...].astype(jnp.float32))
    scale = jnp.exp(local_ref[:note_count] - top) * (dlogit / weight)
    for note in range(note_count):
        scale_rows[note] = jnp.broadcast_to(scale[note : note + 1], (8, labels))
        context_rows[note] = jnp.broadcast_to(context[note : note + 1], (8, labels))
    scale_rows[note_count] = jnp.zeros((8, labels), jnp.float32)
    context_rows[note_count] = jnp.zeros((8, labels), jnp.float32)

    def coef(at, note, mask):
        out = both_ref[at, left] * spread(scale_rows[note], ROWS)
        query = out * (both_ref[at, right] - spread(context_rows[note], ROWS))
        for columns, new in ((left, query), (right, out)):
            if mask is not None:
                new = jnp.where(mask(new.shape), new, coef_ref[at, columns].astype(jnp.float32))
            coef_ref[at, columns] = new.astype(jnp.bfloat16)

    by_note(info_ref, slots, coef)

    def label_copy(side):
        rows = pl.ds(pl.multiple_of(side * labels, labels), labels)
        columns = pl.ds(pl.multiple_of(side * width, width), width)
        return pltpu.make_async_copy(label_ref.at[rows, :], label_hbm.at[:, columns], sems.at[side])

    def label_term(side, carry):
        rows = pl.ds(pl.multiple_of(side * labels, labels), labels)
        label_ref[rows, :] = lax.dot_general(
            coef_ref[:, rows], h_ref[...], (((0,), (0,)), ((), ())), preferred_element_type=jnp.float32
        ).astype(jnp.bfloat16)
        label_copy(side).start()
        return carry

    lax.fori_loop(0, 2, label_term, 0)
    group, core = lax.axis_index("zhi"), lax.axis_index("core")
    part = slots // 2
    half = width // groups // 2

    def token_copies(k):
        rows = pl.ds(pl.multiple_of(k * part, part), part)
        for d in range(groups):
            first = lax.rem(group + d, groups) * (2 * half)
            for side, (ref, at) in enumerate(((mine_hbm, core), (theirs_hbm, 1 - core))):
                columns = pl.ds(pl.multiple_of(first + at * half, half), half)
                yield pltpu.make_async_copy(
                    token_ref.at[rows, columns], ref.at[d, rows, :], sems.at[2 + (k * groups + d) * 2 + side]
                )

    def token_term(k, carry):
        rows = pl.ds(pl.multiple_of(k * part, part), part)
        token_ref[rows, :] = jnp.dot(coef_ref[rows, :], w_ref[...], preferred_element_type=jnp.float32).astype(jnp.bfloat16)
        for copy in token_copies(k):
            copy.start()
        return carry

    lax.fori_loop(0, 2, token_term, 0)
    for k in range(2):
        label_copy(k).wait()
        for copy in token_copies(k):
            copy.wait()


def gradient_terms(info, both, local, a, b, bias, targets, hidden, weights, groups):
    slots, width = hidden.shape
    note_count, labels = targets.shape
    bf16 = jnp.bfloat16
    blocks = pltpu.HBM((groups, slots, width // groups // 2), bf16)
    return pl.pallas_call(
        terms_kernel,
        out_shape=(pltpu.HBM((labels, 2 * width), bf16), blocks, blocks),
        in_specs=[SMEM] + [VMEM] * 8,
        out_specs=(HBM, HBM, HBM),
        scratch_shapes=[pltpu.VMEM((slots, 2 * labels), bf16), pltpu.VMEM((2 * labels, width), bf16),
                        pltpu.VMEM((slots, width), bf16)]
        + [pltpu.VMEM((note_count + 1, 8, labels), jnp.float32)] * 2
        + [pltpu.SemaphoreType.DMA((2 + 4 * groups,))],
        compiler_params=pltpu.CompilerParams(vmem_limit_bytes=24 * MIB),
        name="gradient_terms",
    )(info, both, local, a, b, bias, targets, hidden, weights)


def relay_kernel(mine_ref, given_ref, up_ref, down_ref):
    total = (mine_ref[...].astype(jnp.float32) + given_ref[...].astype(jnp.float32)).astype(jnp.bfloat16)
    for half, ref in enumerate((up_ref, down_ref)):

        @pl.when(pl.program_id(0) == half)
        def _():
            ref[...] = total


def relay_terms(mine, given):
    _, slots, width = mine.shape
    half = slots // 2
    side = pl.BlockSpec((None, half, width), lambda i: (2, i, 0))
    whole = pl.BlockSpec((half, width), lambda i: (0, 0))
    shape = jax.ShapeDtypeStruct((half, width), mine.dtype)
    return pl.pallas_call(
        relay_kernel, out_shape=(shape, shape), grid=(2,), in_specs=[side, side], out_specs=(whole, whole),
        compiler_params=pltpu.CompilerParams(vmem_limit_bytes=8 * MIB), name="relay_terms",
    )(mine, given)


def side_kernel(mine_ref, given_ref, up_ref, down_ref, ahead_ref, behind_ref):
    half = up_ref.shape[0]
    for side, (ref, passed, late) in enumerate(((ahead_ref, up_ref, 0), (behind_ref, down_ref, half))):

        @pl.when(pl.program_id(0) == side)
        def _():
            total = mine_ref[...].astype(jnp.float32) + given_ref[...].astype(jnp.float32)
            ref[half - late : 2 * half - late, :] = total[half - late : 2 * half - late].astype(jnp.bfloat16)
            ref[late : late + half, :] = (total[late : late + half] + passed[...].astype(jnp.float32)).astype(jnp.bfloat16)


def side_terms(mine, given, up, down):
    _, slots, width = mine.shape
    block = pl.BlockSpec((None, slots, width), lambda i: (1 + 2 * i, 0, 0))
    passed = pl.BlockSpec(up.shape, lambda i: (0, 0))
    whole = pl.BlockSpec((slots, width), lambda i: (0, 0))
    shape = jax.ShapeDtypeStruct((slots, width), mine.dtype)
    return pl.pallas_call(
        side_kernel, out_shape=(shape, shape), grid=(2,), in_specs=[block, block, passed, passed], out_specs=(whole, whole),
        compiler_params=pltpu.CompilerParams(vmem_limit_bytes=8 * MIB), name="side_terms",
    )(mine, given, up, down)


def token_sum_kernel(*refs):
    total = sum(ref[...].astype(jnp.float32) for ref in refs[:-1])
    refs[-1][...] = total.astype(refs[-1].dtype)


def token_sum(mine, given, ahead, behind):
    _, slots, width = mine.shape
    steps = 2
    own = pl.BlockSpec((None, slots // steps, width), lambda i: (0, i, 0))
    rows = pl.BlockSpec((slots // steps, width), lambda i: (i, 0))
    return pl.pallas_call(
        token_sum_kernel, out_shape=jax.ShapeDtypeStruct((slots, width), mine.dtype), grid=(steps,),
        in_specs=[own, own, rows, rows], out_specs=rows,
        compiler_params=pltpu.CompilerParams(vmem_limit_bytes=8 * MIB), name="token_sum",
    )(mine, given, ahead, behind)


def label_sum_kernel(other, pieces_ref, out_ref):
    rows, width = out_ref.shape
    part = width // 4
    low = lax.axis_index("zlo")
    at = pl.ds(pl.multiple_of((1 - low if other else low) * rows, rows), rows)
    for k in range(4):
        columns = slice(k * part, (k + 1) * part)
        total = jnp.sum(pieces_ref[:, at, columns].astype(jnp.float32), axis=0)
        out_ref[:, columns] = total.astype(out_ref.dtype)


def label_sum(pieces, other):
    _, rows, width = pieces.shape
    return pl.pallas_call(
        lambda *refs: label_sum_kernel(other, *refs),
        out_shape=jax.ShapeDtypeStruct((rows // 2, width), jnp.bfloat16 if other else jnp.float32),
        in_specs=[VMEM], out_specs=VMEM,
        compiler_params=pltpu.CompilerParams(vmem_limit_bytes=8 * MIB),
        name="label_sum_sent" if other else "label_sum_kept",
    )(pieces)


def shift(value, axis, by):
    size = lax.axis_size(axis)
    return lax.ppermute(value, axis, [(i, (i + by) % size) for i in range(size)])


def shards(hidden, slot_note, queries, out_vectors, label_bias, targets):
    note_count, labels = targets.shape
    width = queries.shape[1]
    f32 = jnp.float32
    both, local, info, held, weights = local_stats(slot_note, hidden, queries, out_vectors, note_count)
    table = local
    for axis in ("x", "y"):
        table = merge([table] + [shift(table, axis, by) for by in range(1, lax.axis_size(axis))])
    other = shift(table, "zlo", 1)
    groups = lax.axis_size("zhi")
    label_term, mine, theirs = gradient_terms(
        info, both, local, table, other, label_bias[None, :], targets, held, weights, groups
    )
    planes = lax.axis_size("y") * lax.axis_size("x")
    given = shift(theirs, "core", 1)
    pieces = lax.all_to_all(label_term.reshape(planes, labels // planes, 2 * width), ("y", "x"), 0, 0)

    up, down = relay_terms(mine, given)
    up, down = shift(up, "zhi", 1), shift(down, "zhi", groups - 1)
    ahead, behind = side_terms(mine, given, up, down)
    token = token_sum(mine, given, shift(ahead, "zhi", 1), shift(behind, "zhi", groups - 1))

    sent = shift(label_sum(pieces, True), "zlo", 1)
    label = label_sum(pieces, False) + sent.astype(f32)
    return token, label[:, :width], label[:, width:]


def solution(mesh):
    split = Mesh(mesh.devices.reshape(4, 2, 4, 4, 2), ("zhi", "core", "y", "x", "zlo"))
    label, seq = ("zhi", "core"), ("y", "x", "zlo")
    in_specs = (P(seq, None), P(seq), P(label, None), P(label, None), P(label), P(None, label))
    out_specs = (P(seq, label), P(label + seq, None), P(label + seq, None))
    return jax.shard_map(shards, mesh=split, in_specs=in_specs, out_specs=out_specs, check_vma=False)
```

```python
import jax
import jax.numpy as jnp
from jax import lax
from jax.experimental import pallas as pl
from jax.experimental.pallas import tpu as pltpu
from jax.sharding import Mesh
from jax.sharding import PartitionSpec as P

MASKED_SCORE = -1e30
LOSS_SCALE = 256.0
ROWS = 128
MIB = 1 << 20


VMEM = pl.BlockSpec(memory_space=pltpu.VMEM)
SMEM = pl.BlockSpec(memory_space=pltpu.SMEM)
HBM = pl.BlockSpec(memory_space=pltpu.HBM)


def in_hbm(value):
    return pltpu.with_memory_space_constraint(value, pltpu.HBM)


RANGES = 16


def note_starts(notes_ref, slots, note_count):
    starts = [jnp.int32(0)]
    for note in range(1, note_count + 1):
        at = jnp.int32(0)
        step = slots // 2
        while step:
            at = jnp.where(notes_ref[at + (step - 1)] < note, at + step, at)
            step //= 2
        starts.append(jnp.where(notes_ref[at] < note, at + 1, at))
    return starts


def fold(values, how):
    rows, labels = values.shape
    return how(values.reshape(rows // 8, 8, labels), axis=0)


def spread(values, rows):
    return jnp.broadcast_to(values[None], (rows // 8,) + values.shape).reshape(rows, values.shape[1])


def by_note(info_ref, slots, one):
    def block(index, carry):
        first = index * ROWS
        at = pl.ds(pl.multiple_of(first, ROWS), ROWS)
        low = info_ref[RANGES + 2 * index]
        high = info_ref[RANGES + 2 * index + 1]

        @pl.when(low == high)
        def _():
            one(at, low, None)

        @pl.when(low != high)
        def _():
            def each(note, carry):
                def mask(shape):
                    row = lax.broadcasted_iota(jnp.int32, shape, 0)
                    return (row >= info_ref[note] - first) & (row < info_ref[note + 1] - first)

                one(at, note, mask)
                return carry

            lax.fori_loop(low, high + 1, each, 0)

        return carry

    lax.fori_loop(0, slots // ROWS, block, 0)


def stats_kernel(notes_hbm, h_hbm, q_hbm, o_hbm, both_ref, table_ref, info_ref, h_ref, w_ref,
                 notes_ref, tops, weights, gains, sems):
    slots = both_ref.shape[0]
    labels = q_hbm.shape[0]
    note_count = table_ref.shape[0] // 3
    part = slots // 2
    copies = [pltpu.make_async_copy(notes_hbm, notes_ref, sems.at[0]),
              pltpu.make_async_copy(q_hbm, w_ref.at[pl.ds(0, labels), :], sems.at[1]),
              pltpu.make_async_copy(o_hbm, w_ref.at[pl.ds(labels, labels), :], sems.at[2])]
    for k in range(2):
        rows = pl.ds(k * part, part)
        copies.append(pltpu.make_async_copy(h_hbm.at[rows, :], h_ref.at[rows, :], sems.at[3 + k]))
    for k in (0, 3, 1, 2, 4):
        copies[k].start()
    tops[...] = jnp.full(tops.shape, MASKED_SCORE, jnp.float32)
    weights[...] = jnp.zeros(weights.shape, jnp.float32)
    gains[...] = jnp.zeros(gains.shape, jnp.float32)
    copies[0].wait()
    for note, start in enumerate(note_starts(notes_ref, slots, note_count)):
        info_ref[note] = start
    info_ref[note_count + 1] = jnp.int32(slots)
    for k in range(slots // ROWS):
        info_ref[RANGES + 2 * k] = notes_ref[k * ROWS]
        info_ref[RANGES + 2 * k + 1] = notes_ref[k * ROWS + ROWS - 1]
    for k in (3, 1, 2, 4):
        copies[k].wait()

    def product(k, carry):
        rows = pl.ds(pl.multiple_of(k * part, part), part)
        both_ref[rows, :] = lax.dot_general(
            h_ref[rows, :], w_ref[...], (((1,), (1,)), ((), ())), preferred_element_type=jnp.float32
        )
        return carry

    lax.fori_loop(0, 2, product, 0)
    left, right = slice(0, labels), slice(labels, 2 * labels)

    def top(at, note, mask):
        scores = both_ref[at, left]
        if mask is not None:
            scores = jnp.where(mask(scores.shape), scores, MASKED_SCORE)
        tops[note] = jnp.maximum(tops[note], fold(scores, jnp.max))

    by_note(info_ref, slots, top)
    for note in range(note_count):
        most = jnp.max(tops[note], axis=0, keepdims=True)
        table_ref[note : note + 1, :] = most
        tops[note] = jnp.broadcast_to(most, (8, labels))
    tops[note_count] = jnp.full((8, labels), -MASKED_SCORE, jnp.float32)

    def exponent(at, note, mask):
        scores = both_ref[at, left]
        expo = jnp.exp(scores - spread(tops[note], ROWS))
        if mask is None:
            both_ref[at, left] = expo
        else:
            inside = mask(scores.shape)
            both_ref[at, left] = jnp.where(inside, expo, scores)
            expo = jnp.where(inside, expo, 0.0)
        weights[note] += fold(expo, jnp.sum)
        gains[note] += fold(expo * both_ref[at, right], jnp.sum)

    by_note(info_ref, slots, exponent)
    for note in range(note_count):
        table_ref[note_count + note : note_count + note + 1, :] = jnp.sum(weights[note], axis=0, keepdims=True)
        table_ref[2 * note_count + note : 2 * note_count + note + 1, :] = jnp.sum(gains[note], axis=0, keepdims=True)


def local_stats(notes, hidden, queries, out_vectors, note_count):
    slots, width = hidden.shape
    labels = queries.shape[0]
    return pl.pallas_call(
        stats_kernel,
        out_shape=(
            pltpu.VMEM((slots, 2 * labels), jnp.float32),
            jax.ShapeDtypeStruct((3 * note_count, labels), jnp.float32),
            jax.ShapeDtypeStruct((RANGES + 2 * (slots // ROWS),), jnp.int32),
            pltpu.VMEM(hidden.shape, hidden.dtype),
            pltpu.VMEM((2 * labels, width), queries.dtype),
        ),
        in_specs=[HBM] * 4,
        out_specs=(VMEM, VMEM, SMEM, VMEM, VMEM),
        scratch_shapes=[pltpu.SMEM((slots,), jnp.int32)]
        + [pltpu.VMEM((note_count + 1, 8, labels), jnp.float32)] * 3
        + [pltpu.SemaphoreType.DMA((5,))],
        compiler_params=pltpu.CompilerParams(vmem_limit_bytes=24 * MIB),
        name="local_stats",
    )(*map(in_hbm, (notes, hidden, queries, out_vectors)))


def merged(tables):
    n = tables[0].shape[0] // 3
    top = tables[0][:n]
    for table in tables[1:]:
        top = jnp.maximum(top, table[:n])
    weight = gain = 0.0
    for table in tables:
        scale = jnp.exp(table[:n] - top)
        weight = weight + scale * table[n : 2 * n]
        gain = gain + scale * table[2 * n :]
    return top, weight, gain


def merge_kernel(*refs):
    n = refs[0].shape[0] // 3
    out = refs[-1]
    out[:n], out[n : 2 * n], out[2 * n :] = merged([ref[...] for ref in refs[:-1]])


def merge(tables):
    return pl.pallas_call(
        merge_kernel,
        out_shape=jax.ShapeDtypeStruct(tables[0].shape, jnp.float32),
        in_specs=[VMEM] * len(tables),
        out_specs=VMEM,
        compiler_params=pltpu.CompilerParams(vmem_limit_bytes=2 * MIB),
        name="merge",
    )(*tables)


def terms_kernel(info_ref, both_ref, local_ref, a_ref, b_ref, bias_ref, target_ref, h_ref, w_ref,
                 label_hbm, mine_hbm, theirs_hbm, coef_ref, label_ref, token_ref, scale_rows, context_rows, sems):
    slots, labels = both_ref.shape[0], bias_ref.shape[1]
    width = h_ref.shape[1]
    note_count = target_ref.shape[0]
    groups = mine_hbm.shape[0]
    left, right = slice(0, labels), slice(labels, 2 * labels)
    top, weight, gain = merged([a_ref[...], b_ref[...]])
    context = gain / weight
    chance = 1.0 / (1.0 + jnp.exp(-(context + bias_ref[...])))
    dlogit = LOSS_SCALE * (chance - target_ref[...].astype(jnp.float32))
    scale = jnp.exp(local_ref[:note_count] - top) * (dlogit / weight)
    for note in range(note_count):
        scale_rows[note] = jnp.broadcast_to(scale[note : note + 1], (8, labels))
        context_rows[note] = jnp.broadcast_to(context[note : note + 1], (8, labels))
    scale_rows[note_count] = jnp.zeros((8, labels), jnp.float32)
    context_rows[note_count] = jnp.zeros((8, labels), jnp.float32)

    def coef(at, note, mask):
        out = both_ref[at, left] * spread(scale_rows[note], ROWS)
        query = out * (both_ref[at, right] - spread(context_rows[note], ROWS))
        for columns, new in ((left, query), (right, out)):
            if mask is not None:
                new = jnp.where(mask(new.shape), new, coef_ref[at, columns].astype(jnp.float32))
            coef_ref[at, columns] = new.astype(jnp.bfloat16)

    by_note(info_ref, slots, coef)

    def label_copy(side):
        rows = pl.ds(pl.multiple_of(side * labels, labels), labels)
        columns = pl.ds(pl.multiple_of(side * width, width), width)
        return pltpu.make_async_copy(label_ref.at[rows, :], label_hbm.at[:, columns], sems.at[side])

    def label_term(side, carry):
        rows = pl.ds(pl.multiple_of(side * labels, labels), labels)
        label_ref[rows, :] = lax.dot_general(
            coef_ref[:, rows], h_ref[...], (((0,), (0,)), ((), ())), preferred_element_type=jnp.float32
        ).astype(jnp.bfloat16)
        label_copy(side).start()
        return carry

    lax.fori_loop(0, 2, label_term, 0)
    group, core = lax.axis_index("zhi"), lax.axis_index("core")
    part = slots // 2
    half = width // groups // 2

    def token_copies(k):
        rows = pl.ds(pl.multiple_of(k * part, part), part)
        for d in range(groups):
            first = lax.rem(group + d, groups) * (2 * half)
            for side, (ref, at) in enumerate(((mine_hbm, core), (theirs_hbm, 1 - core))):
                columns = pl.ds(pl.multiple_of(first + at * half, half), half)
                yield pltpu.make_async_copy(
                    token_ref.at[rows, columns], ref.at[d, rows, :], sems.at[2 + (k * groups + d) * 2 + side]
                )

    def token_term(k, carry):
        rows = pl.ds(pl.multiple_of(k * part, part), part)
        token_ref[rows, :] = jnp.dot(coef_ref[rows, :], w_ref[...], preferred_element_type=jnp.float32).astype(jnp.bfloat16)
        for copy in token_copies(k):
            copy.start()
        return carry

    lax.fori_loop(0, 2, token_term, 0)
    for k in range(2):
        label_copy(k).wait()
        for copy in token_copies(k):
            copy.wait()


def gradient_terms(info, both, local, a, b, bias, targets, hidden, weights, groups):
    slots, width = hidden.shape
    note_count, labels = targets.shape
    bf16 = jnp.bfloat16
    blocks = pltpu.HBM((groups, slots, width // groups // 2), bf16)
    return pl.pallas_call(
        terms_kernel,
        out_shape=(pltpu.HBM((labels, 2 * width), bf16), blocks, blocks),
        in_specs=[SMEM] + [VMEM] * 8,
        out_specs=(HBM, HBM, HBM),
        scratch_shapes=[pltpu.VMEM((slots, 2 * labels), bf16), pltpu.VMEM((2 * labels, width), bf16),
                        pltpu.VMEM((slots, width), bf16)]
        + [pltpu.VMEM((note_count + 1, 8, labels), jnp.float32)] * 2
        + [pltpu.SemaphoreType.DMA((2 + 4 * groups,))],
        compiler_params=pltpu.CompilerParams(vmem_limit_bytes=24 * MIB),
        name="gradient_terms",
    )(info, both, local, a, b, bias, targets, hidden, weights)


def relay_kernel(mine_ref, given_ref, up_ref, down_ref):
    total = (mine_ref[...].astype(jnp.float32) + given_ref[...].astype(jnp.float32)).astype(jnp.bfloat16)
    for half, ref in enumerate((up_ref, down_ref)):

        @pl.when(pl.program_id(0) == half)
        def _():
            ref[...] = total


def relay_terms(mine, given):
    _, slots, width = mine.shape
    half = slots // 2
    side = pl.BlockSpec((None, half, width), lambda i: (2, i, 0))
    whole = pl.BlockSpec((half, width), lambda i: (0, 0))
    shape = jax.ShapeDtypeStruct((half, width), mine.dtype)
    return pl.pallas_call(
        relay_kernel, out_shape=(shape, shape), grid=(2,), in_specs=[side, side], out_specs=(whole, whole),
        compiler_params=pltpu.CompilerParams(vmem_limit_bytes=8 * MIB), name="relay_terms",
    )(mine, given)


def side_kernel(mine_ref, given_ref, up_ref, down_ref, ahead_ref, behind_ref):
    half = up_ref.shape[0]
    for side, (ref, passed, late) in enumerate(((ahead_ref, up_ref, 0), (behind_ref, down_ref, half))):

        @pl.when(pl.program_id(0) == side)
        def _():
            total = mine_ref[...].astype(jnp.float32) + given_ref[...].astype(jnp.float32)
            ref[half - late : 2 * half - late, :] = total[half - late : 2 * half - late].astype(jnp.bfloat16)
            ref[late : late + half, :] = (total[late : late + half] + passed[...].astype(jnp.float32)).astype(jnp.bfloat16)


def side_terms(mine, given, up, down):
    _, slots, width = mine.shape
    block = pl.BlockSpec((None, slots, width), lambda i: (1 + 2 * i, 0, 0))
    passed = pl.BlockSpec(up.shape, lambda i: (0, 0))
    whole = pl.BlockSpec((slots, width), lambda i: (0, 0))
    shape = jax.ShapeDtypeStruct((slots, width), mine.dtype)
    return pl.pallas_call(
        side_kernel, out_shape=(shape, shape), grid=(2,), in_specs=[block, block, passed, passed], out_specs=(whole, whole),
        compiler_params=pltpu.CompilerParams(vmem_limit_bytes=8 * MIB), name="side_terms",
    )(mine, given, up, down)


def token_sum_kernel(*refs):
    total = sum(ref[...].astype(jnp.float32) for ref in refs[:-1])
    refs[-1][...] = total.astype(refs[-1].dtype)


def token_sum(mine, given, ahead, behind):
    _, slots, width = mine.shape
    steps = 2
    own = pl.BlockSpec((None, slots // steps, width), lambda i: (0, i, 0))
    rows = pl.BlockSpec((slots // steps, width), lambda i: (i, 0))
    return pl.pallas_call(
        token_sum_kernel, out_shape=jax.ShapeDtypeStruct((slots, width), mine.dtype), grid=(steps,),
        in_specs=[own, own, rows, rows], out_specs=rows,
        compiler_params=pltpu.CompilerParams(vmem_limit_bytes=8 * MIB), name="token_sum",
    )(mine, given, ahead, behind)


def label_sum_kernel(other, pieces_ref, out_ref):
    rows, width = out_ref.shape
    part = width // 4
    low = lax.axis_index("zlo")
    at = pl.ds(pl.multiple_of((1 - low if other else low) * rows, rows), rows)
    for k in range(4):
        columns = slice(k * part, (k + 1) * part)
        total = jnp.sum(pieces_ref[:, at, columns].astype(jnp.float32), axis=0)
        out_ref[:, columns] = total.astype(out_ref.dtype)


def label_sum(pieces, other):
    _, rows, width = pieces.shape
    return pl.pallas_call(
        lambda *refs: label_sum_kernel(other, *refs),
        out_shape=jax.ShapeDtypeStruct((rows // 2, width), jnp.bfloat16 if other else jnp.float32),
        in_specs=[VMEM], out_specs=VMEM,
        compiler_params=pltpu.CompilerParams(vmem_limit_bytes=8 * MIB),
        name="label_sum_sent" if other else "label_sum_kept",
    )(pieces)


def shift(value, axis, by):
    size = lax.axis_size(axis)
    return lax.ppermute(value, axis, [(i, (i + by) % size) for i in range(size)])


def shards(hidden, slot_note, queries, out_vectors, label_bias, targets):
    note_count, labels = targets.shape
    width = queries.shape[1]
    f32 = jnp.float32
    both, local, info, held, weights = local_stats(slot_note, hidden, queries, out_vectors, note_count)
    table = local
    for axis in ("x", "y"):
        table = merge([table] + [shift(table, axis, by) for by in range(1, lax.axis_size(axis))])
    other = shift(table, "zlo", 1)
    groups = lax.axis_size("zhi")
    label_term, mine, theirs = gradient_terms(
        info, both, local, table, other, label_bias[None, :], targets, held, weights, groups
    )
    planes = lax.axis_size("y") * lax.axis_size("x")
    given = shift(theirs, "core", 1)
    pieces = lax.all_to_all(label_term.reshape(planes, labels // planes, 2 * width), ("y", "x"), 0, 0)

    up, down = relay_terms(mine, given)
    up, down = shift(up, "zhi", 1), shift(down, "zhi", groups - 1)
    ahead, behind = side_terms(mine, given, up, down)
    token = token_sum(mine, given, shift(ahead, "zhi", 1), shift(behind, "zhi", groups - 1))

    sent = shift(label_sum(pieces, True), "zlo", 1)
    label = label_sum(pieces, False) + sent.astype(f32)
    return token, label[:, :width], label[:, width:]


def solution(mesh):
    split = Mesh(mesh.devices.reshape(4, 2, 4, 4, 2), ("zhi", "core", "y", "x", "zlo"))
    label, seq = ("zhi", "core"), ("y", "x", "zlo")
    in_specs = (P(seq, None), P(seq), P(label, None), P(label, None), P(label), P(None, label))
    out_specs = (P(seq, label), P(label + seq, None), P(label + seq, None))
    return jax.shard_map(shards, mesh=split, in_specs=in_specs, out_specs=out_specs, check_vma=False)
```

```python
import jax
import jax.numpy as jnp
from jax import lax
from jax.experimental import pallas as pl
from jax.experimental.pallas import tpu as pltpu
from jax.sharding import Mesh
from jax.sharding import PartitionSpec as P

MASKED_SCORE = -1e30
LOSS_SCALE = 256.0
ROWS = 128
FINE = 32
MIB = 1 << 20


VMEM = pl.BlockSpec(memory_space=pltpu.VMEM)
SMEM = pl.BlockSpec(memory_space=pltpu.SMEM)
HBM = pl.BlockSpec(memory_space=pltpu.HBM)


def in_hbm(value):
    return pltpu.with_memory_space_constraint(value, pltpu.HBM)


RANGES = 16


def note_starts(notes_ref, slots, note_count):
    starts = [jnp.int32(0)]
    for note in range(1, note_count + 1):
        at = jnp.int32(0)
        step = slots // 2
        while step:
            at = jnp.where(notes_ref[at + (step - 1)] < note, at + step, at)
            step //= 2
        starts.append(jnp.where(notes_ref[at] < note, at + 1, at))
    return starts


def fold(values, how):
    rows, labels = values.shape
    return how(values.reshape(rows // 8, 8, labels), axis=0)


def spread(values, rows):
    return jnp.broadcast_to(values[None], (rows // 8,) + values.shape).reshape(rows, values.shape[1])


def by_note(info_ref, slots, one):
    smaller = ROWS // FINE

    def block(index, carry):
        low = info_ref[RANGES + 2 * smaller * index]
        high = info_ref[RANGES + 2 * smaller * (index + 1) - 1]

        @pl.when(low == high)
        def _():
            one(pl.ds(pl.multiple_of(index * ROWS, ROWS), ROWS), ROWS, low, None)

        @pl.when(low != high)
        def _():
            lax.fori_loop(index * smaller, (index + 1) * smaller, fine, 0)

        return carry

    def fine(index, carry):
        first = index * FINE
        at = pl.ds(pl.multiple_of(first, FINE), FINE)
        low = info_ref[RANGES + 2 * index]
        high = info_ref[RANGES + 2 * index + 1]

        @pl.when(low == high)
        def _():
            one(at, FINE, low, None)

        @pl.when(low != high)
        def _():
            def each(note, carry):
                def mask(shape):
                    row = lax.broadcasted_iota(jnp.int32, shape, 0)
                    return (row >= info_ref[note] - first) & (row < info_ref[note + 1] - first)

                one(at, FINE, note, mask)
                return carry

            lax.fori_loop(low, high + 1, each, 0)

        return carry

    lax.fori_loop(0, slots // ROWS, block, 0)


def stats_kernel(notes_hbm, h_hbm, q_hbm, o_hbm, both_ref, table_ref, info_ref, h_ref, w_ref,
                 notes_ref, tops, weights, gains, sems):
    slots = both_ref.shape[0]
    labels = q_hbm.shape[0]
    note_count = table_ref.shape[0] // 3
    part = slots // 2
    copies = [pltpu.make_async_copy(notes_hbm, notes_ref, sems.at[0]),
              pltpu.make_async_copy(q_hbm, w_ref.at[pl.ds(0, labels), :], sems.at[1]),
              pltpu.make_async_copy(o_hbm, w_ref.at[pl.ds(labels, labels), :], sems.at[2])]
    for k in range(2):
        rows = pl.ds(k * part, part)
        copies.append(pltpu.make_async_copy(h_hbm.at[rows, :], h_ref.at[rows, :], sems.at[3 + k]))
    for k in (0, 3, 1, 2, 4):
        copies[k].start()
    tops[...] = jnp.full(tops.shape, MASKED_SCORE, jnp.float32)
    weights[...] = jnp.zeros(weights.shape, jnp.float32)
    gains[...] = jnp.zeros(gains.shape, jnp.float32)
    copies[0].wait()
    for note, start in enumerate(note_starts(notes_ref, slots, note_count)):
        info_ref[note] = start
    info_ref[note_count + 1] = jnp.int32(slots)
    for k in range(slots // FINE):
        info_ref[RANGES + 2 * k] = notes_ref[k * FINE]
        info_ref[RANGES + 2 * k + 1] = notes_ref[k * FINE + FINE - 1]
    for k in (3, 1, 2, 4):
        copies[k].wait()

    def product(k, carry):
        rows = pl.ds(pl.multiple_of(k * part, part), part)
        both_ref[rows, :] = lax.dot_general(
            h_ref[rows, :], w_ref[...], (((1,), (1,)), ((), ())), preferred_element_type=jnp.float32
        )
        return carry

    lax.fori_loop(0, 2, product, 0)
    left, right = slice(0, labels), slice(labels, 2 * labels)

    def top(at, count, note, mask):
        scores = both_ref[at, left]
        if mask is not None:
            scores = jnp.where(mask(scores.shape), scores, MASKED_SCORE)
        tops[note] = jnp.maximum(tops[note], fold(scores, jnp.max))

    by_note(info_ref, slots, top)
    for note in range(note_count):
        most = jnp.max(tops[note], axis=0, keepdims=True)
        table_ref[note : note + 1, :] = most
        tops[note] = jnp.broadcast_to(most, (8, labels))
    tops[note_count] = jnp.full((8, labels), -MASKED_SCORE, jnp.float32)

    def exponent(at, count, note, mask):
        scores = both_ref[at, left]
        expo = jnp.exp(scores - spread(tops[note], count))
        if mask is None:
            both_ref[at, left] = expo
        else:
            inside = mask(scores.shape)
            both_ref[at, left] = jnp.where(inside, expo, scores)
            expo = jnp.where(inside, expo, 0.0)
        weights[note] += fold(expo, jnp.sum)
        gains[note] += fold(expo * both_ref[at, right], jnp.sum)

    by_note(info_ref, slots, exponent)
    for note in range(note_count):
        table_ref[note_count + note : note_count + note + 1, :] = jnp.sum(weights[note], axis=0, keepdims=True)
        table_ref[2 * note_count + note : 2 * note_count + note + 1, :] = jnp.sum(gains[note], axis=0, keepdims=True)


def local_stats(notes, hidden, queries, out_vectors, note_count):
    slots, width = hidden.shape
    labels = queries.shape[0]
    return pl.pallas_call(
        stats_kernel,
        out_shape=(
            pltpu.VMEM((slots, 2 * labels), jnp.float32),
            jax.ShapeDtypeStruct((3 * note_count, labels), jnp.float32),
            jax.ShapeDtypeStruct((RANGES + 2 * (slots // FINE),), jnp.int32),
            pltpu.VMEM(hidden.shape, hidden.dtype),
            pltpu.VMEM((2 * labels, width), queries.dtype),
        ),
        in_specs=[HBM] * 4,
        out_specs=(VMEM, VMEM, SMEM, VMEM, VMEM),
        scratch_shapes=[pltpu.SMEM((slots,), jnp.int32)]
        + [pltpu.VMEM((note_count + 1, 8, labels), jnp.float32)] * 3
        + [pltpu.SemaphoreType.DMA((5,))],
        compiler_params=pltpu.CompilerParams(vmem_limit_bytes=24 * MIB),
        name="local_stats",
    )(*map(in_hbm, (notes, hidden, queries, out_vectors)))


def merged(tables):
    n = tables[0].shape[0] // 3
    top = tables[0][:n]
    for table in tables[1:]:
        top = jnp.maximum(top, table[:n])
    weight = gain = 0.0
    for table in tables:
        scale = jnp.exp(table[:n] - top)
        weight = weight + scale * table[n : 2 * n]
        gain = gain + scale * table[2 * n :]
    return top, weight, gain


def merge_kernel(*refs):
    n = refs[0].shape[0] // 3
    out = refs[-1]
    out[:n], out[n : 2 * n], out[2 * n :] = merged([ref[...] for ref in refs[:-1]])


def merge(tables):
    return pl.pallas_call(
        merge_kernel,
        out_shape=jax.ShapeDtypeStruct(tables[0].shape, jnp.float32),
        in_specs=[VMEM] * len(tables),
        out_specs=VMEM,
        compiler_params=pltpu.CompilerParams(vmem_limit_bytes=2 * MIB),
        name="merge",
    )(*tables)


def terms_kernel(info_ref, both_ref, local_ref, a_ref, b_ref, bias_ref, target_ref, h_ref, w_ref,
                 label_hbm, mine_hbm, theirs_hbm, coef_ref, label_ref, token_ref, scale_rows, context_rows, sems):
    slots, labels = both_ref.shape[0], bias_ref.shape[1]
    width = h_ref.shape[1]
    note_count = target_ref.shape[0]
    groups = mine_hbm.shape[0]
    left, right = slice(0, labels), slice(labels, 2 * labels)
    top, weight, gain = merged([a_ref[...], b_ref[...]])
    context = gain / weight
    chance = 1.0 / (1.0 + jnp.exp(-(context + bias_ref[...])))
    dlogit = LOSS_SCALE * (chance - target_ref[...].astype(jnp.float32))
    scale = jnp.exp(local_ref[:note_count] - top) * (dlogit / weight)
    for note in range(note_count):
        scale_rows[note] = jnp.broadcast_to(scale[note : note + 1], (8, labels))
        context_rows[note] = jnp.broadcast_to(context[note : note + 1], (8, labels))
    scale_rows[note_count] = jnp.zeros((8, labels), jnp.float32)
    context_rows[note_count] = jnp.zeros((8, labels), jnp.float32)

    def coef(at, count, note, mask):
        out = both_ref[at, left] * spread(scale_rows[note], count)
        query = out * (both_ref[at, right] - spread(context_rows[note], count))
        for columns, new in ((left, query), (right, out)):
            if mask is not None:
                new = jnp.where(mask(new.shape), new, coef_ref[at, columns].astype(jnp.float32))
            coef_ref[at, columns] = new.astype(jnp.bfloat16)

    by_note(info_ref, slots, coef)

    def label_copy(side):
        rows = pl.ds(pl.multiple_of(side * labels, labels), labels)
        columns = pl.ds(pl.multiple_of(side * width, width), width)
        return pltpu.make_async_copy(label_ref.at[rows, :], label_hbm.at[:, columns], sems.at[side])

    def label_term(side, carry):
        rows = pl.ds(pl.multiple_of(side * labels, labels), labels)
        label_ref[rows, :] = lax.dot_general(
            coef_ref[:, rows], h_ref[...], (((0,), (0,)), ((), ())), preferred_element_type=jnp.float32
        ).astype(jnp.bfloat16)
        label_copy(side).start()
        return carry

    lax.fori_loop(0, 2, label_term, 0)
    group, core = lax.axis_index("zhi"), lax.axis_index("core")
    part = slots // 2
    half = width // groups // 2

    def token_copies(k):
        rows = pl.ds(pl.multiple_of(k * part, part), part)
        for d in range(groups):
            first = lax.rem(group + d, groups) * (2 * half)
            for side, (ref, at) in enumerate(((mine_hbm, core), (theirs_hbm, 1 - core))):
                columns = pl.ds(pl.multiple_of(first + at * half, half), half)
                yield pltpu.make_async_copy(
                    token_ref.at[rows, columns], ref.at[d, rows, :], sems.at[2 + (k * groups + d) * 2 + side]
                )

    def token_term(k, carry):
        rows = pl.ds(pl.multiple_of(k * part, part), part)
        token_ref[rows, :] = jnp.dot(coef_ref[rows, :], w_ref[...], preferred_element_type=jnp.float32).astype(jnp.bfloat16)
        for copy in token_copies(k):
            copy.start()
        return carry

    lax.fori_loop(0, 2, token_term, 0)
    for k in range(2):
        label_copy(k).wait()
        for copy in token_copies(k):
            copy.wait()


def gradient_terms(info, both, local, a, b, bias, targets, hidden, weights, groups):
    slots, width = hidden.shape
    note_count, labels = targets.shape
    bf16 = jnp.bfloat16
    blocks = pltpu.HBM((groups, slots, width // groups // 2), bf16)
    return pl.pallas_call(
        terms_kernel,
        out_shape=(pltpu.HBM((labels, 2 * width), bf16), blocks, blocks),
        in_specs=[SMEM] + [VMEM] * 8,
        out_specs=(HBM, HBM, HBM),
        scratch_shapes=[pltpu.VMEM((slots, 2 * labels), bf16), pltpu.VMEM((2 * labels, width), bf16),
                        pltpu.VMEM((slots, width), bf16)]
        + [pltpu.VMEM((note_count + 1, 8, labels), jnp.float32)] * 2
        + [pltpu.SemaphoreType.DMA((2 + 4 * groups,))],
        compiler_params=pltpu.CompilerParams(vmem_limit_bytes=24 * MIB),
        name="gradient_terms",
    )(info, both, local, a, b, bias, targets, hidden, weights)


def relay_kernel(mine_ref, given_ref, up_ref, down_ref):
    total = (mine_ref[...].astype(jnp.float32) + given_ref[...].astype(jnp.float32)).astype(jnp.bfloat16)
    for half, ref in enumerate((up_ref, down_ref)):

        @pl.when(pl.program_id(0) == half)
        def _():
            ref[...] = total


def relay_terms(mine, given):
    _, slots, width = mine.shape
    half = slots // 2
    side = pl.BlockSpec((None, half, width), lambda i: (2, i, 0))
    whole = pl.BlockSpec((half, width), lambda i: (0, 0))
    shape = jax.ShapeDtypeStruct((half, width), mine.dtype)
    return pl.pallas_call(
        relay_kernel, out_shape=(shape, shape), grid=(2,), in_specs=[side, side], out_specs=(whole, whole),
        compiler_params=pltpu.CompilerParams(vmem_limit_bytes=8 * MIB), name="relay_terms",
    )(mine, given)


def side_kernel(mine_ref, given_ref, up_ref, down_ref, ahead_ref, behind_ref):
    half = up_ref.shape[0]
    for side, (ref, passed, late) in enumerate(((ahead_ref, up_ref, 0), (behind_ref, down_ref, half))):

        @pl.when(pl.program_id(0) == side)
        def _():
            total = mine_ref[...].astype(jnp.float32) + given_ref[...].astype(jnp.float32)
            ref[half - late : 2 * half - late, :] = total[half - late : 2 * half - late].astype(jnp.bfloat16)
            ref[late : late + half, :] = (total[late : late + half] + passed[...].astype(jnp.float32)).astype(jnp.bfloat16)


def side_terms(mine, given, up, down):
    _, slots, width = mine.shape
    block = pl.BlockSpec((None, slots, width), lambda i: (1 + 2 * i, 0, 0))
    passed = pl.BlockSpec(up.shape, lambda i: (0, 0))
    whole = pl.BlockSpec((slots, width), lambda i: (0, 0))
    shape = jax.ShapeDtypeStruct((slots, width), mine.dtype)
    return pl.pallas_call(
        side_kernel, out_shape=(shape, shape), grid=(2,), in_specs=[block, block, passed, passed], out_specs=(whole, whole),
        compiler_params=pltpu.CompilerParams(vmem_limit_bytes=8 * MIB), name="side_terms",
    )(mine, given, up, down)


def final_kernel(mine_ref, given_ref, ahead_ref, behind_ref, kept_ref, sent_ref, token_ref, query_ref, out_ref):
    total = sum(ref[...].astype(jnp.float32) for ref in (mine_ref, given_ref, ahead_ref, behind_ref))
    token_ref[...] = total.astype(token_ref.dtype)

    @pl.when(pl.program_id(0) == 0)
    def _():
        width = query_ref.shape[1]
        label = kept_ref[...] + sent_ref[...].astype(jnp.float32)
        query_ref[...] = label[:, :width]
        out_ref[...] = label[:, width:]


def final_sums(mine, given, ahead, behind, kept, sent):
    _, slots, width = mine.shape
    rows, both = kept.shape
    steps = 2
    own = pl.BlockSpec((None, slots // steps, width), lambda i: (0, i, 0))
    part = pl.BlockSpec((slots // steps, width), lambda i: (i, 0))
    label = pl.BlockSpec((rows, both), lambda i: (0, 0))
    side = pl.BlockSpec((rows, both // 2), lambda i: (0, 0))
    grad = jax.ShapeDtypeStruct((rows, both // 2), jnp.float32)
    return pl.pallas_call(
        final_kernel, out_shape=(jax.ShapeDtypeStruct((slots, width), mine.dtype), grad, grad), grid=(steps,),
        in_specs=[own, own, part, part, label, label], out_specs=(part, side, side),
        compiler_params=pltpu.CompilerParams(vmem_limit_bytes=8 * MIB), name="final_sums",
    )(mine, given, ahead, behind, kept, sent)


def label_sum_kernel(other, pieces_ref, out_ref):
    rows, width = out_ref.shape
    part = width // 4
    low = lax.axis_index("zlo")
    at = pl.ds(pl.multiple_of((1 - low if other else low) * rows, rows), rows)
    for k in range(4):
        columns = slice(k * part, (k + 1) * part)
        total = jnp.sum(pieces_ref[:, at, columns].astype(jnp.float32), axis=0)
        out_ref[:, columns] = total.astype(out_ref.dtype)


def label_sum(pieces, other):
    _, rows, width = pieces.shape
    return pl.pallas_call(
        lambda *refs: label_sum_kernel(other, *refs),
        out_shape=jax.ShapeDtypeStruct((rows // 2, width), jnp.bfloat16 if other else jnp.float32),
        in_specs=[VMEM], out_specs=VMEM,
        compiler_params=pltpu.CompilerParams(vmem_limit_bytes=8 * MIB),
        name="label_sum_sent" if other else "label_sum_kept",
    )(pieces)


def shift(value, axis, by):
    size = lax.axis_size(axis)
    return lax.ppermute(value, axis, [(i, (i + by) % size) for i in range(size)])


def shards(hidden, slot_note, queries, out_vectors, label_bias, targets):
    note_count, labels = targets.shape
    width = queries.shape[1]
    both, local, info, held, weights = local_stats(slot_note, hidden, queries, out_vectors, note_count)
    table = local
    for axis in ("x", "y"):
        table = merge([table] + [shift(table, axis, by) for by in range(1, lax.axis_size(axis))])
    other = shift(table, "zlo", 1)
    groups = lax.axis_size("zhi")
    label_term, mine, theirs = gradient_terms(
        info, both, local, table, other, label_bias[None, :], targets, held, weights, groups
    )
    planes = lax.axis_size("y") * lax.axis_size("x")
    given = shift(theirs, "core", 1)
    pieces = lax.all_to_all(label_term.reshape(planes, labels // planes, 2 * width), ("y", "x"), 0, 0)

    up, down = relay_terms(mine, given)
    up, down = shift(up, "zhi", 1), shift(down, "zhi", groups - 1)
    ahead, behind = side_terms(mine, given, up, down)
    ahead, behind = shift(ahead, "zhi", 1), shift(behind, "zhi", groups - 1)
    sent = shift(label_sum(pieces, True), "zlo", 1)
    return final_sums(mine, given, ahead, behind, label_sum(pieces, False), sent)


def solution(mesh):
    split = Mesh(mesh.devices.reshape(4, 2, 4, 4, 2), ("zhi", "core", "y", "x", "zlo"))
    label, seq = ("zhi", "core"), ("y", "x", "zlo")
    in_specs = (P(seq, None), P(seq), P(label, None), P(label, None), P(label), P(None, label))
    out_specs = (P(seq, label), P(label + seq, None), P(label + seq, None))
    return jax.shard_map(shards, mesh=split, in_specs=in_specs, out_specs=out_specs, check_vma=False)
```

```python
import jax
import jax.numpy as jnp
from jax import lax
from jax.experimental import pallas as pl
from jax.experimental.pallas import tpu as pltpu
from jax.sharding import Mesh
from jax.sharding import PartitionSpec as P

MASKED_SCORE = -1e30
LOSS_SCALE = 256.0
ROWS = 128
FINE = 32
MIB = 1 << 20


VMEM = pl.BlockSpec(memory_space=pltpu.VMEM)
SMEM = pl.BlockSpec(memory_space=pltpu.SMEM)
HBM = pl.BlockSpec(memory_space=pltpu.HBM)


def in_hbm(value):
    return pltpu.with_memory_space_constraint(value, pltpu.HBM)


RANGES = 16


def note_starts(notes_ref, slots, note_count):
    starts = [jnp.int32(0)]
    for note in range(1, note_count + 1):
        at = jnp.int32(0)
        step = slots // 2
        while step:
            at = jnp.where(notes_ref[at + (step - 1)] < note, at + step, at)
            step //= 2
        starts.append(jnp.where(notes_ref[at] < note, at + 1, at))
    return starts


def fold(values, how):
    rows, labels = values.shape
    return how(values.reshape(rows // 8, 8, labels), axis=0)


def spread(values, rows):
    return jnp.broadcast_to(values[None], (rows // 8,) + values.shape).reshape(rows, values.shape[1])


def by_note(info_ref, slots, one):
    smaller = ROWS // FINE

    def block(index, carry):
        low = info_ref[RANGES + 2 * smaller * index]
        high = info_ref[RANGES + 2 * smaller * (index + 1) - 1]

        @pl.when(low == high)
        def _():
            one(pl.ds(pl.multiple_of(index * ROWS, ROWS), ROWS), ROWS, low, None)

        @pl.when(low != high)
        def _():
            lax.fori_loop(index * smaller, (index + 1) * smaller, fine, 0)

        return carry

    def fine(index, carry):
        first = index * FINE
        at = pl.ds(pl.multiple_of(first, FINE), FINE)
        low = info_ref[RANGES + 2 * index]
        high = info_ref[RANGES + 2 * index + 1]

        @pl.when(low == high)
        def _():
            one(at, FINE, low, None)

        @pl.when(low != high)
        def _():
            def each(note, carry):
                def mask(shape):
                    row = lax.broadcasted_iota(jnp.int32, shape, 0)
                    return (row >= info_ref[note] - first) & (row < info_ref[note + 1] - first)

                one(at, FINE, note, mask)
                return carry

            lax.fori_loop(low, high + 1, each, 0)

        return carry

    lax.fori_loop(0, slots // ROWS, block, 0)


def stats_kernel(notes_hbm, h_hbm, q_hbm, o_hbm, both_ref, table_ref, info_ref, h_ref, w_ref,
                 notes_ref, tops, weights, gains, sems):
    slots = both_ref.shape[0]
    labels = q_hbm.shape[0]
    note_count = table_ref.shape[0] // 3
    part = slots // 2
    copies = [pltpu.make_async_copy(notes_hbm, notes_ref, sems.at[0]),
              pltpu.make_async_copy(q_hbm, w_ref.at[pl.ds(0, labels), :], sems.at[1]),
              pltpu.make_async_copy(o_hbm, w_ref.at[pl.ds(labels, labels), :], sems.at[2])]
    for k in range(2):
        rows = pl.ds(k * part, part)
        copies.append(pltpu.make_async_copy(h_hbm.at[rows, :], h_ref.at[rows, :], sems.at[3 + k]))
    for k in (0, 3, 1, 2, 4):
        copies[k].start()
    tops[...] = jnp.full(tops.shape, MASKED_SCORE, jnp.float32)
    weights[...] = jnp.zeros(weights.shape, jnp.float32)
    gains[...] = jnp.zeros(gains.shape, jnp.float32)
    copies[0].wait()
    for note, start in enumerate(note_starts(notes_ref, slots, note_count)):
        info_ref[note] = start
    info_ref[note_count + 1] = jnp.int32(slots)
    for k in range(slots // FINE):
        info_ref[RANGES + 2 * k] = notes_ref[k * FINE]
        info_ref[RANGES + 2 * k + 1] = notes_ref[k * FINE + FINE - 1]
    for k in (3, 1, 2):
        copies[k].wait()

    def product(k, carry):
        @pl.when(k == 1)
        def _():
            copies[4].wait()

        rows = pl.ds(pl.multiple_of(k * part, part), part)
        both_ref[rows, :] = lax.dot_general(
            h_ref[rows, :], w_ref[...], (((1,), (1,)), ((), ())), preferred_element_type=jnp.float32
        )
        return carry

    lax.fori_loop(0, 2, product, 0)
    left, right = slice(0, labels), slice(labels, 2 * labels)

    def top(at, count, note, mask):
        scores = both_ref[at, left]
        if mask is not None:
            scores = jnp.where(mask(scores.shape), scores, MASKED_SCORE)
        tops[note] = jnp.maximum(tops[note], fold(scores, jnp.max))

    by_note(info_ref, slots, top)
    for note in range(note_count):
        most = jnp.max(tops[note], axis=0, keepdims=True)
        table_ref[note : note + 1, :] = most
        tops[note] = jnp.broadcast_to(most, (8, labels))
    tops[note_count] = jnp.full((8, labels), -MASKED_SCORE, jnp.float32)

    def exponent(at, count, note, mask):
        scores = both_ref[at, left]
        expo = jnp.exp(scores - spread(tops[note], count))
        if mask is None:
            both_ref[at, left] = expo
        else:
            inside = mask(scores.shape)
            both_ref[at, left] = jnp.where(inside, expo, scores)
            expo = jnp.where(inside, expo, 0.0)
        weights[note] += fold(expo, jnp.sum)
        gains[note] += fold(expo * both_ref[at, right], jnp.sum)

    by_note(info_ref, slots, exponent)
    for note in range(note_count):
        table_ref[note_count + note : note_count + note + 1, :] = jnp.sum(weights[note], axis=0, keepdims=True)
        table_ref[2 * note_count + note : 2 * note_count + note + 1, :] = jnp.sum(gains[note], axis=0, keepdims=True)


def local_stats(notes, hidden, queries, out_vectors, note_count):
    slots, width = hidden.shape
    labels = queries.shape[0]
    return pl.pallas_call(
        stats_kernel,
        out_shape=(
            pltpu.VMEM((slots, 2 * labels), jnp.float32),
            jax.ShapeDtypeStruct((3 * note_count, labels), jnp.float32),
            jax.ShapeDtypeStruct((RANGES + 2 * (slots // FINE),), jnp.int32),
            pltpu.VMEM(hidden.shape, hidden.dtype),
            pltpu.VMEM((2 * labels, width), queries.dtype),
        ),
        in_specs=[HBM] * 4,
        out_specs=(VMEM, VMEM, SMEM, VMEM, VMEM),
        scratch_shapes=[pltpu.SMEM((slots,), jnp.int32)]
        + [pltpu.VMEM((note_count + 1, 8, labels), jnp.float32)] * 3
        + [pltpu.SemaphoreType.DMA((5,))],
        compiler_params=pltpu.CompilerParams(vmem_limit_bytes=24 * MIB),
        name="local_stats",
    )(*map(in_hbm, (notes, hidden, queries, out_vectors)))


def merged(tables):
    n = tables[0].shape[0] // 3
    top = tables[0][:n]
    for table in tables[1:]:
        top = jnp.maximum(top, table[:n])
    weight = gain = 0.0
    for table in tables:
        scale = jnp.exp(table[:n] - top)
        weight = weight + scale * table[n : 2 * n]
        gain = gain + scale * table[2 * n :]
    return top, weight, gain


def merge_kernel(*refs):
    n = refs[0].shape[0] // 3
    out = refs[-1]
    out[:n], out[n : 2 * n], out[2 * n :] = merged([ref[...] for ref in refs[:-1]])


def merge(tables):
    return pl.pallas_call(
        merge_kernel,
        out_shape=jax.ShapeDtypeStruct(tables[0].shape, jnp.float32),
        in_specs=[VMEM] * len(tables),
        out_specs=VMEM,
        compiler_params=pltpu.CompilerParams(vmem_limit_bytes=2 * MIB),
        name="merge",
    )(*tables)


def terms_kernel(info_ref, both_ref, local_ref, a_ref, b_ref, bias_ref, target_ref, h_ref, w_ref,
                 label_hbm, mine_hbm, theirs_hbm, coef_ref, label_ref, token_ref, scale_rows, context_rows, sems):
    slots, labels = both_ref.shape[0], bias_ref.shape[1]
    width = h_ref.shape[1]
    note_count = target_ref.shape[0]
    groups = mine_hbm.shape[0]
    left, right = slice(0, labels), slice(labels, 2 * labels)
    top, weight, gain = merged([a_ref[...], b_ref[...]])
    context = gain / weight
    chance = 1.0 / (1.0 + jnp.exp(-(context + bias_ref[...])))
    dlogit = LOSS_SCALE * (chance - target_ref[...].astype(jnp.float32))
    scale = jnp.exp(local_ref[:note_count] - top) * (dlogit / weight)
    for note in range(note_count):
        scale_rows[note] = jnp.broadcast_to(scale[note : note + 1], (8, labels))
        context_rows[note] = jnp.broadcast_to(context[note : note + 1], (8, labels))
    scale_rows[note_count] = jnp.zeros((8, labels), jnp.float32)
    context_rows[note_count] = jnp.zeros((8, labels), jnp.float32)

    def coef(at, count, note, mask):
        out = both_ref[at, left] * spread(scale_rows[note], count)
        query = out * (both_ref[at, right] - spread(context_rows[note], count))
        for columns, new in ((left, query), (right, out)):
            if mask is not None:
                new = jnp.where(mask(new.shape), new, coef_ref[at, columns].astype(jnp.float32))
            coef_ref[at, columns] = new.astype(jnp.bfloat16)

    by_note(info_ref, slots, coef)

    def label_copy(side):
        rows = pl.ds(pl.multiple_of(side * labels, labels), labels)
        columns = pl.ds(pl.multiple_of(side * width, width), width)
        return pltpu.make_async_copy(label_ref.at[rows, :], label_hbm.at[:, columns], sems.at[side])

    def label_term(side, carry):
        rows = pl.ds(pl.multiple_of(side * labels, labels), labels)
        label_ref[rows, :] = lax.dot_general(
            coef_ref[:, rows], h_ref[...], (((0,), (0,)), ((), ())), preferred_element_type=jnp.float32
        ).astype(jnp.bfloat16)
        label_copy(side).start()
        return carry

    lax.fori_loop(0, 2, label_term, 0)
    group, core = lax.axis_index("zhi"), lax.axis_index("core")
    part = slots // 2
    half = width // groups // 2

    def token_copies(k):
        rows = pl.ds(pl.multiple_of(k * part, part), part)
        for d in range(groups):
            first = lax.rem(group + d, groups) * (2 * half)
            for side, (ref, at) in enumerate(((mine_hbm, core), (theirs_hbm, 1 - core))):
                columns = pl.ds(pl.multiple_of(first + at * half, half), half)
                yield pltpu.make_async_copy(
                    token_ref.at[rows, columns], ref.at[d, rows, :], sems.at[2 + (k * groups + d) * 2 + side]
                )

    def token_term(k, carry):
        rows = pl.ds(pl.multiple_of(k * part, part), part)
        token_ref[rows, :] = jnp.dot(coef_ref[rows, :], w_ref[...], preferred_element_type=jnp.float32).astype(jnp.bfloat16)
        for copy in token_copies(k):
            copy.start()
        return carry

    lax.fori_loop(0, 2, token_term, 0)
    for k in range(2):
        label_copy(k).wait()
        for copy in token_copies(k):
            copy.wait()


def gradient_terms(info, both, local, a, b, bias, targets, hidden, weights, groups):
    slots, width = hidden.shape
    note_count, labels = targets.shape
    bf16 = jnp.bfloat16
    blocks = pltpu.HBM((groups, slots, width // groups // 2), bf16)
    return pl.pallas_call(
        terms_kernel,
        out_shape=(pltpu.HBM((labels, 2 * width), bf16), blocks, blocks),
        in_specs=[SMEM] + [VMEM] * 8,
        out_specs=(HBM, HBM, HBM),
        scratch_shapes=[pltpu.VMEM((slots, 2 * labels), bf16), pltpu.VMEM((2 * labels, width), bf16),
                        pltpu.VMEM((slots, width), bf16)]
        + [pltpu.VMEM((note_count + 1, 8, labels), jnp.float32)] * 2
        + [pltpu.SemaphoreType.DMA((2 + 4 * groups,))],
        compiler_params=pltpu.CompilerParams(vmem_limit_bytes=24 * MIB),
        name="gradient_terms",
    )(info, both, local, a, b, bias, targets, hidden, weights)


def relay_kernel(mine_ref, given_ref, up_ref, down_ref):
    total = (mine_ref[...].astype(jnp.float32) + given_ref[...].astype(jnp.float32)).astype(jnp.bfloat16)
    for half, ref in enumerate((up_ref, down_ref)):

        @pl.when(pl.program_id(0) == half)
        def _():
            ref[...] = total


def relay_terms(mine, given):
    _, slots, width = mine.shape
    half = slots // 2
    side = pl.BlockSpec((None, half, width), lambda i: (2, i, 0))
    whole = pl.BlockSpec((half, width), lambda i: (0, 0))
    shape = jax.ShapeDtypeStruct((half, width), mine.dtype)
    return pl.pallas_call(
        relay_kernel, out_shape=(shape, shape), grid=(2,), in_specs=[side, side], out_specs=(whole, whole),
        compiler_params=pltpu.CompilerParams(vmem_limit_bytes=8 * MIB), name="relay_terms",
    )(mine, given)


def side_kernel(mine_ref, given_ref, up_ref, down_ref, ahead_ref, behind_ref):
    half = up_ref.shape[0]
    for side, (ref, passed, late) in enumerate(((ahead_ref, up_ref, 0), (behind_ref, down_ref, half))):

        @pl.when(pl.program_id(0) == side)
        def _():
            total = mine_ref[...].astype(jnp.float32) + given_ref[...].astype(jnp.float32)
            ref[half - late : 2 * half - late, :] = total[half - late : 2 * half - late].astype(jnp.bfloat16)
            ref[late : late + half, :] = (total[late : late + half] + passed[...].astype(jnp.float32)).astype(jnp.bfloat16)


def side_terms(mine, given, up, down):
    _, slots, width = mine.shape
    block = pl.BlockSpec((None, slots, width), lambda i: (1 + 2 * i, 0, 0))
    passed = pl.BlockSpec(up.shape, lambda i: (0, 0))
    whole = pl.BlockSpec((slots, width), lambda i: (0, 0))
    shape = jax.ShapeDtypeStruct((slots, width), mine.dtype)
    return pl.pallas_call(
        side_kernel, out_shape=(shape, shape), grid=(2,), in_specs=[block, block, passed, passed], out_specs=(whole, whole),
        compiler_params=pltpu.CompilerParams(vmem_limit_bytes=8 * MIB), name="side_terms",
    )(mine, given, up, down)


def final_kernel(mine_ref, given_ref, ahead_ref, behind_ref, kept_ref, sent_ref, token_ref, query_ref, out_ref):
    total = sum(ref[...].astype(jnp.float32) for ref in (mine_ref, given_ref, ahead_ref, behind_ref))
    token_ref[...] = total.astype(token_ref.dtype)

    @pl.when(pl.program_id(0) == 0)
    def _():
        width = query_ref.shape[1]
        label = kept_ref[...] + sent_ref[...].astype(jnp.float32)
        query_ref[...] = label[:, :width]
        out_ref[...] = label[:, width:]


def final_sums(mine, given, ahead, behind, kept, sent):
    _, slots, width = mine.shape
    rows, both = kept.shape
    steps = 2
    own = pl.BlockSpec((None, slots // steps, width), lambda i: (0, i, 0))
    part = pl.BlockSpec((slots // steps, width), lambda i: (i, 0))
    label = pl.BlockSpec((rows, both), lambda i: (0, 0))
    side = pl.BlockSpec((rows, both // 2), lambda i: (0, 0))
    grad = jax.ShapeDtypeStruct((rows, both // 2), jnp.float32)
    return pl.pallas_call(
        final_kernel, out_shape=(jax.ShapeDtypeStruct((slots, width), mine.dtype), grad, grad), grid=(steps,),
        in_specs=[own, own, part, part, label, label], out_specs=(part, side, side),
        compiler_params=pltpu.CompilerParams(vmem_limit_bytes=8 * MIB), name="final_sums",
    )(mine, given, ahead, behind, kept, sent)


def label_sum_kernel(other, pieces_ref, out_ref):
    rows, width = out_ref.shape
    part = width // 4
    low = lax.axis_index("zlo")
    at = pl.ds(pl.multiple_of((1 - low if other else low) * rows, rows), rows)
    for k in range(4):
        columns = slice(k * part, (k + 1) * part)
        total = jnp.sum(pieces_ref[:, at, columns].astype(jnp.float32), axis=0)
        out_ref[:, columns] = total.astype(out_ref.dtype)


def label_sum(pieces, other):
    _, rows, width = pieces.shape
    return pl.pallas_call(
        lambda *refs: label_sum_kernel(other, *refs),
        out_shape=jax.ShapeDtypeStruct((rows // 2, width), jnp.bfloat16 if other else jnp.float32),
        in_specs=[VMEM], out_specs=VMEM,
        compiler_params=pltpu.CompilerParams(vmem_limit_bytes=8 * MIB),
        name="label_sum_sent" if other else "label_sum_kept",
    )(pieces)


def shift(value, axis, by):
    size = lax.axis_size(axis)
    return lax.ppermute(value, axis, [(i, (i + by) % size) for i in range(size)])


def shards(hidden, slot_note, queries, out_vectors, label_bias, targets):
    note_count, labels = targets.shape
    width = queries.shape[1]
    both, local, info, held, weights = local_stats(slot_note, hidden, queries, out_vectors, note_count)
    table = local
    for axis in ("x", "y"):
        table = merge([table] + [shift(table, axis, by) for by in range(1, lax.axis_size(axis))])
    other = shift(table, "zlo", 1)
    groups = lax.axis_size("zhi")
    label_term, mine, theirs = gradient_terms(
        info, both, local, table, other, label_bias[None, :], targets, held, weights, groups
    )
    planes = lax.axis_size("y") * lax.axis_size("x")
    given = shift(theirs, "core", 1)
    pieces = lax.all_to_all(label_term.reshape(planes, labels // planes, 2 * width), ("y", "x"), 0, 0)

    up, down = relay_terms(mine, given)
    up, down = shift(up, "zhi", 1), shift(down, "zhi", groups - 1)
    ahead, behind = side_terms(mine, given, up, down)
    ahead, behind = shift(ahead, "zhi", 1), shift(behind, "zhi", groups - 1)
    sent = shift(label_sum(pieces, True), "zlo", 1)
    return final_sums(mine, given, ahead, behind, label_sum(pieces, False), sent)


def solution(mesh):
    split = Mesh(mesh.devices.reshape(4, 2, 4, 4, 2), ("zhi", "core", "y", "x", "zlo"))
    label, seq = ("zhi", "core"), ("y", "x", "zlo")
    in_specs = (P(seq, None), P(seq), P(label, None), P(label, None), P(label), P(None, label))
    out_specs = (P(seq, label), P(label + seq, None), P(label + seq, None))
    return jax.shard_map(shards, mesh=split, in_specs=in_specs, out_specs=out_specs, check_vma=False)
```
